128 devices in a mesh: dom: 32 (over x_lo, z, y), rep: 4 (over x_hi, core).
Axes of the slice: x: 4 (x_hi: 2, x_lo: 2; x = x_hi * 2 + x_lo), y: 4, z: 4, core: 2. Of those that a mesh axis runs over, the one named last changes fastest.
Arguments:
- features: bfloat16 [49152, 256], P('dom'), may hold values from -6 to 6
- tile_weights: bfloat16 [32, 4, 8, 88, 128, 128], P('dom', 'rep'), may hold values from 0 to 0.0115356445
- tile_rows: int32 [32, 4, 8, 88], P('dom', 'rep'), may hold values from 0 to 11, as said below
- tile_cols: int32 [32, 4, 8, 88], P('dom', 'rep'), may hold values from 0 to 11, as said below
- tile_counts: int32 [32, 4, 8], P('dom', 'rep'), may hold values from 1 to 88, as said below
- weight_self: bfloat16 [256, 256], replicated, may hold values from -0.375 to 0.375
- weight_neigh: bfloat16 [256, 256], replicated, may hold values from -0.375 to 0.375
- cotangent: bfloat16 [49152, 256], P(('dom', 'rep')), may hold values from -0.026977539 to 0.026977539
Outputs:
- out: bfloat16 [49152, 256], P(('dom', 'rep'))
- grad_self: float32 [256, 256], replicated
- grad_neigh: float32 [256, 256], replicated
The draws below stay inside these ranges and needn't reach their ends.
Inputs may be any that keep to these rules, and one draw needn't show every extreme that they name: For each p, r, s the first tile_counts[p, r, s] slots name distinct pairs (tile_rows, tile_cols); slots from tile_counts[p, r, s] on are unused. `tile_cols`: see tile_rows. `tile_counts`: some device fills all 88 slots of some column step.
All inputs are finite; a program needn't handle non-finite values.
Results may differ from the reference program's by a relative error of at most 0.0052.
Values may be sent and summed in bfloat16 or wider, within the bound.
A program may use at most 128 MiB of HBM per device.

```python
import jax
import jax.numpy as jnp
from jax import lax

F = 256
TILE = 128
RT = 12
KS = 88
BLOCKS = 32
GROUPS = 4
STEPS = 8
NODES = 49152
N_DOM = 32
N_REP = 4


def tile_positions(key):
    base = jax.random.fold_in(key, 7)
    keys = jax.random.split(base, BLOCKS * GROUPS * STEPS)

    def permute_one(single_key):
        return jax.random.permutation(single_key, RT * RT)[:KS]
    chosen = jax.vmap(permute_one)(keys)
    return chosen.reshape(BLOCKS, GROUPS, STEPS, KS).astype(jnp.int32)


def draw_tile_rows(key, part):
    return tile_positions(key) // RT


def draw_tile_cols(key, part):
    return tile_positions(key) % RT


def draw_tile_counts(key, part):
    base = jax.random.fold_in(key, 3)
    first_key, second_key, third_key = jax.random.split(base, 3)
    divisor = jax.random.randint(first_key, (BLOCKS, GROUPS, 1), 1, 5)
    jitter = jax.random.randint(second_key, (BLOCKS, GROUPS, STEPS), 0, max(KS // 8, 1))
    counts = jnp.maximum(KS // divisor - jitter, 1).astype(jnp.int32)
    total = BLOCKS * GROUPS * STEPS
    chosen = jax.random.randint(third_key, (), 0, total)
    flat = jnp.where(jnp.arange(total) == chosen, KS, counts.reshape(total))
    return flat.reshape(BLOCKS, GROUPS, STEPS).astype(jnp.int32)


def block_levels(own_key, extent, pieces, smallest, top_value):
    loudness, own = 1.0, jax.random.fold_in(own_key, 6)
    for axis_at, parts in pieces:
        draws = jnp.exp(jax.random.uniform(jax.random.fold_in(own, axis_at), (parts,), jnp.float32, smallest / len(pieces), top_value / len(pieces)))
        loudness = loudness * jnp.repeat(draws, extent[axis_at] // parts).reshape([-1 if axis == axis_at else 1 for axis in range(len(extent))])
    return loudness


def bell_draw(own_key, shape, spread, limit, cuts=(), kind=jnp.bfloat16):
    entries = spread * jax.random.normal(own_key, shape, jnp.float32)
    if cuts:
        entries = entries * block_levels(own_key, shape, cuts, -0.22, 0.18)
    return jnp.clip(entries, -limit, limit).astype(kind)


def setup_inputs(seed: int = 0) -> dict:
    seeds = jax.random.split(jax.random.key(seed), 9)
    return {
        "features": bell_draw(seeds[0], (NODES, F), 1.0, 6.0, ((0, 32),)),
        "tile_weights": jnp.clip(0.0115356445 * jax.random.uniform(seeds[1], (BLOCKS, GROUPS, STEPS, KS, TILE, TILE), jnp.float32) ** block_levels(seeds[1], (BLOCKS, GROUPS, STEPS, KS, TILE, TILE), ((0, 32), (1, 4)), -0.2, 0.2), 0.0, 0.0115356445).astype(jnp.bfloat16),
        "tile_rows": draw_tile_rows(jax.random.fold_in(seeds[8], 71), 0),
        "tile_cols": draw_tile_cols(jax.random.fold_in(seeds[8], 71), 0),
        "tile_counts": draw_tile_counts(jax.random.fold_in(seeds[8], 71), 0),
        "weight_self": bell_draw(seeds[5], (F, F), F ** -0.5, 0.375),
        "weight_neigh": bell_draw(seeds[6], (F, F), F ** -0.5, 0.375),
        "cotangent": bell_draw(seeds[7], (NODES, F), (1.0 / NODES ** 0.5), 0.026977539, ((0, 128),)),
    }


def block_aggregate(features, tile_weights, tile_rows, tile_cols, tile_counts, block_index):
    tiled = features.reshape(N_DOM, RT, TILE, F)
    group_ids = jnp.arange(N_REP, dtype=jnp.int32)[:, None]
    step_ids = jnp.arange(STEPS, dtype=jnp.int32)[None, :]
    column_block = (block_index + group_ids * STEPS + step_ids - STEPS // 2 + N_DOM) % N_DOM
    cols_now = tile_cols[block_index]
    picked = tiled[column_block[:, :, None], cols_now].astype(jnp.float32)
    live_slots = (jnp.arange(KS, dtype=jnp.int32)[None, None, :] < tile_counts[block_index][:, :, None])
    weights_now = tile_weights[block_index].astype(jnp.float32) * live_slots.astype(jnp.float32)[:, :, :, None, None]
    product = jnp.einsum('gskij,gskjf->gskif', weights_now, picked)
    rows_now = tile_rows[block_index].reshape(N_REP * STEPS * KS)
    partial_value = jnp.zeros((RT, TILE, F), product.dtype)
    partial_value = partial_value.at[rows_now].add(product.reshape(N_REP * STEPS * KS, TILE, F))
    return partial_value


def reference(features, tile_weights, tile_rows, tile_cols, tile_counts, weight_self, weight_neigh, cotangent):
    def one_block(block_index):
        return block_aggregate(features, tile_weights, tile_rows, tile_cols, tile_counts, block_index)

    summed = lax.map(one_block, jnp.arange(N_DOM, dtype=jnp.int32))
    aggregate = summed.reshape(NODES, F).astype(jnp.bfloat16)
    pre = jnp.dot(features, weight_self, preferred_element_type=jnp.float32)
    pre = pre + jnp.dot(aggregate, weight_neigh, preferred_element_type=jnp.float32)
    output = jax.nn.silu(pre).astype(jnp.bfloat16)
    sigmoid = jax.nn.sigmoid(pre)
    slope = (cotangent.astype(jnp.float32) * sigmoid * (1.0 + pre * (1.0 - sigmoid))).astype(jnp.bfloat16)
    grad_self = jnp.dot(features.T, slope, preferred_element_type=jnp.float32)
    grad_neigh = jnp.dot(aggregate.T, slope, preferred_element_type=jnp.float32)
    return (output, grad_self, grad_neigh)
```

```python
import functools

import jax
import jax.numpy as jnp
from jax import lax
from jax.experimental import pallas as pl
from jax.experimental.pallas import tpu as pltpu
from jax.sharding import PartitionSpec as P

MESH = pl.DeviceIdType.MESH
BLOCKS = 32
STEPS = 8
SLOTS = 88
TILE = 128
RT = 12
WIDTH = 256
SUBS = 3
SUB = 256
ROWS = 1536
QUARTER = 384


def where_am_i():
    p = lax.axis_index("dom")
    rep = lax.axis_index("rep")
    copy, core = rep // 2, rep % 2
    g = (p + 16 * copy) % BLOCKS
    return copy, core, g


def device(copy, g, core):
    return ((g + 16 * copy) % BLOCKS, 2 * copy + core)


def at(z, y):
    return (z % 8) * 4 + y


def aggregate_kernel(
    slots,
    features,
    weights,
    weight_self,
    weight_neigh,
    cotangent,
    out_ref,
    self_ref,
    neigh_ref,
    wbuf,
    fbuf,
    obuf,
    acc,
    r1buf,
    r1src,
    r2src,
    r2buf,
    w_sem,
    own_sem,
    f_sem,
    o_sem,
    r1_sem,
    r2_sem,
    s_swap,
    s_y,
    s_yr,
    s_zd,
    s_zu,
    s_rd,
    s_ru,
    s_x,
    s_x2,
    s_o,
    s_r1,
    s_r2,
):
    k, c, g = where_am_i()
    z, y = g // 4, g % 4
    first, mine_no = k, 1 - k

    here = device(k, g, c)
    other_core = device(k, g, 1 - c)
    other_copy = device(1 - k, g, c)
    y_up, y_down = (y + 1) % 4, (y + 3) % 4
    to_y_up = device(k, at(z, y_up), c)
    to_y_down = device(k, at(z, y_down), c)
    to_z_down = device(k, at(z + 7, y), c)
    to_z_up = device(k, at(z + 1, y), c)
    to_z_flip = device(k, at(z + 5, y), c)
    to_z_flip_back = device(k, at(z + 3, y), c)
    to_twin = device(k, (g + 16) % BLOCKS, c)
    to_rep = device(1 - k, (g + 16) % BLOCKS, c)
    del here

    for step in range(STEPS):
        pltpu.make_async_copy(
            weights.at[pl.ds(step * SLOTS, SLOTS)], wbuf.at[pl.ds(step * SLOTS, SLOTS)], w_sem.at[step]
        ).start()

    barrier = pltpu.get_barrier_semaphore()
    partners = (
        other_core,
        other_copy,
        to_y_up,
        to_y_down,
        to_z_down,
        to_z_up,
        to_z_flip,
        to_z_flip_back,
        to_twin,
        to_rep,
    )
    for partner in partners:
        pl.semaphore_signal(barrier, inc=1, device_id=partner, device_id_type=MESH)
    wbuf[STEPS * SLOTS] = jnp.zeros((TILE, TILE), wbuf.dtype)
    pl.semaphore_wait(barrier, len(partners))

    def push(slot_from, sub_from, slot_to, send_sem, target):
        pltpu.make_async_remote_copy(
            src_ref=fbuf.at[slot_from, sub_from],
            dst_ref=fbuf.at[slot_to, sub_from],
            send_sem=send_sem,
            recv_sem=f_sem.at[slot_to, sub_from],
            device_id=target,
            device_id_type=MESH,
        ).start()

    def arrived(slot, sub):
        pltpu.make_async_copy(fbuf.at[slot, sub], fbuf.at[slot, sub], f_sem.at[slot, sub]).wait()

    def sent(sem):
        pltpu.make_async_copy(fbuf.at[0, 0], fbuf.at[0, 0], sem).wait()

    def give_core(slot):
        half = slot // STEPS
        pltpu.make_async_remote_copy(
            src_ref=fbuf.at[slot],
            dst_ref=obuf.at[slot % STEPS],
            send_sem=s_o.at[slot % STEPS],
            recv_sem=o_sem.at[slot % STEPS],
            device_id=other_core,
            device_id_type=MESH,
        ).start()
        del half

    def swap(sub, target):
        pltpu.make_async_remote_copy(
            src_ref=features.at[c, sub],
            dst_ref=fbuf.at[4, sub],
            send_sem=s_swap.at[sub],
            recv_sem=f_sem.at[4, sub],
            device_id=target,
            device_id_type=MESH,
        ).start()

    sender = jnp.logical_or(jnp.logical_and(k == 0, c == 0), jnp.logical_and(k == 1, c == 1))

    @pl.when(jnp.logical_and(k == 0, c == 0))
    def _():
        for sub in range(SUBS):
            swap(sub, other_copy)

    @pl.when(jnp.logical_and(k == 1, c == 1))
    def _():
        for sub in range(SUBS):
            swap(sub, to_twin)

    @pl.when(k == 0)
    def _():
        for sub in range(SUBS):
            pltpu.make_async_copy(features.at[c, sub], fbuf.at[4, sub], f_sem.at[4, sub]).start()

    def z_sends(slot, block_y, j):
        delta = block_y - y
        for n, sub in enumerate((first, 2)):
            push(slot, sub, 8 + delta, s_zd.at[j, n], to_z_down)
        above = delta >= 0
        z_to = jnp.where(above, z + 1, z + 5)
        target = device(k, at(z_to, y), c)
        for n, sub in enumerate((first, 2)):
            push(slot, sub, (delta + 16) % 16, s_zu.at[j, n], target)

    for sub in range(SUBS):
        arrived(4, sub)
        push(4, sub, 4 + y - y_up, s_y.at[0, sub], to_y_up)
        push(4, sub, 4 + y - y_down, s_y.at[1, sub], to_y_down)
    z_sends(4, y, 0)

    @pl.when(c == 1)
    def _():
        give_core(4)

    from_up = 4 + y_up - y
    from_down = 4 + y_down - y
    for sub in range(SUBS):
        arrived(from_down, sub)
        if sub != 1:
            push(from_down, sub, 4 + y_down - y_up, s_yr.at[sub], to_y_up)
        arrived(from_up, sub)
        if sub == 1:
            push(from_up, sub, 4 + y_up - y_down, s_yr.at[sub], to_y_down)
    z_sends(from_up, y_up, 1)
    z_sends(from_down, y_down, 3)

    @pl.when(c == 1)
    def _():
        give_core(from_up)
        give_core(from_down)

    opposite = (y + 2) % 4
    from_opposite = 4 + opposite - y
    for sub in range(SUBS):
        arrived(from_opposite, sub)
    z_sends(from_opposite, opposite, 2)

    @pl.when(c == 1)
    def _():
        give_core(from_opposite)

    acc[...] = jnp.zeros_like(acc)
    for step in range(STEPS):
        pltpu.make_async_copy(
            weights.at[pl.ds(step * SLOTS, SLOTS)], wbuf.at[pl.ds(step * SLOTS, SLOTS)], w_sem.at[step]
        ).wait()

    group = 3

    def multiply(slot):
        step = slot % STEPS
        pltpu.make_async_copy(obuf.at[step], obuf.at[step], o_sem.at[step]).wait()
        half_cols = RT // 2

        def rows_of(r, carry):
            base = step * (RT * RT) + r * (group * RT)
            total = None
            for ref, at_slot, side in ((fbuf, slot, c), (obuf, step, 1 - c)):
                stacked = []
                for n in range(group):
                    tiles = [
                        wbuf[slots[base + n * RT + half_cols * side + i]] for i in range(half_cols)
                    ]
                    stacked.append(jnp.concatenate(tiles, axis=1))
                lhs = jnp.concatenate(stacked, axis=0)
                rhs = ref[at_slot].reshape(SUBS * SUB, WIDTH)
                term = jnp.dot(lhs, rhs, preferred_element_type=jnp.float32)
                total = term if total is None else total + term
            window = pl.ds(pl.multiple_of(r * (group * TILE), group * TILE), group * TILE)
            acc[window, :] += total
            return carry

        lax.fori_loop(0, RT // group, rows_of, 0)

    def order(i):
        return i + i // 2 - 2 * (i // 3)

    def delta_of(i):
        return (y + order(i)) % 4 - y

    def first_pass(i, carry):
        delta = delta_of(i)
        above = 8 + delta
        below = (delta + 16) % 16
        far = 12 + delta
        arrived(above, first)
        push(above, first, far, s_rd.at[i], to_z_down)
        push(above, first, above, s_x.at[0, i], other_copy)
        arrived(above, 2)
        arrived(below, first)
        push(below, first, below, s_x.at[1, i], other_copy)
        arrived(below, 2)
        z_to = jnp.where(delta >= 0, z + 5, z + 1)
        push(below, 2, far, s_ru.at[i], device(k, at(z_to, y), c))

        @pl.when(c == 0)
        def _():
            multiply(4 + delta)

        return carry

    lax.fori_loop(0, 4, first_pass, 0)

    def second_pass(i, carry):
        delta = delta_of(i)
        above = 8 + delta
        below = (delta + 16) % 16
        far = 12 + delta
        arrived(far, first)
        push(far, first, far, s_x2.at[i], other_copy)
        arrived(above, mine_no)
        arrived(below, mine_no)
        mine = jnp.where(above // STEPS == c, above, below)
        theirs = above + below - mine
        give_core(theirs)
        multiply(mine)
        return carry

    lax.fori_loop(0, 4, second_pass, 0)

    def third_pass(i, carry):
        far = 12 + delta_of(i)
        arrived(far, 2)
        arrived(far, mine_no)

        @pl.when(c == 0)
        def _():
            give_core(far)

        @pl.when(c == 1)
        def _():
            multiply(far)

        return carry

    lax.fori_loop(0, 4, third_pass, 0)

    for part in range(2):
        start = pl.multiple_of((2 * part + 1 - c) * QUARTER, QUARTER)
        r1src[part] = acc[pl.ds(start, QUARTER), :]
        pltpu.make_async_remote_copy(
            src_ref=r1src.at[part],
            dst_ref=r1buf.at[part],
            send_sem=s_r1.at[part],
            recv_sem=r1_sem.at[part],
            device_id=other_core,
            device_id_type=MESH,
        ).start()

    for sem in [s_y.at[d, s] for d in range(2) for s in range(SUBS)] + [s_yr.at[s] for s in range(SUBS)]:
        sent(sem)
    for j in range(4):
        for n in range(2):
            sent(s_zd.at[j, n])
            sent(s_zu.at[j, n])
            sent(s_x.at[n, j])
        sent(s_rd.at[j])
        sent(s_ru.at[j])
        sent(s_x2.at[j])
    for step in range(STEPS):
        pltpu.make_async_copy(obuf.at[step], obuf.at[step], s_o.at[step]).wait()

    @pl.when(sender)
    def _():
        for sub in range(SUBS):
            sent(s_swap.at[sub])

    for part in range(2):
        pltpu.make_async_copy(r1buf.at[part], r1buf.at[part], r1_sem.at[part]).wait()

    away = pl.multiple_of((2 * (1 - k) + c) * QUARTER, QUARTER)
    r2src[...] = (acc[pl.ds(away, QUARTER), :] + r1buf[1 - k]).astype(r2src.dtype)
    cross = pltpu.make_async_remote_copy(
        src_ref=r2src,
        dst_ref=r2buf,
        send_sem=s_r2,
        recv_sem=r2_sem,
        device_id=to_rep,
        device_id_type=MESH,
    )
    cross.start()
    home = pl.multiple_of((2 * k + c) * QUARTER, QUARTER)
    kept = acc[pl.ds(home, QUARTER), :] + r1buf[k]
    own = features.reshape(ROWS, WIDTH)[pl.ds(home, QUARTER), :]
    pre = jnp.dot(own, weight_self[...], preferred_element_type=jnp.float32)
    cross.wait()
    aggregate = (kept + r2buf[...].astype(jnp.float32)).astype(jnp.bfloat16)
    pre = pre + jnp.dot(aggregate, weight_neigh[...], preferred_element_type=jnp.float32)
    sigmoid = jax.nn.sigmoid(pre)
    out_ref[...] = (pre * sigmoid).astype(out_ref.dtype)
    slope = (cotangent[...].astype(jnp.float32) * sigmoid * (1.0 + pre * (1.0 - sigmoid))).astype(
        jnp.bfloat16
    )
    contract = (((0,), (0,)), ((), ()))
    self_ref[...] = lax.dot_general(own, slope, contract, preferred_element_type=jnp.float32)
    neigh_ref[...] = lax.dot_general(aggregate, slope, contract, preferred_element_type=jnp.float32)
    for part in range(2):
        pltpu.make_async_copy(r1src.at[part], r1src.at[part], s_r1.at[part]).wait()


def slot_table(rows, cols, counts):
    steps, slots = rows.shape
    key = rows * RT + cols
    live = jnp.arange(slots, dtype=jnp.int32)[None, :] < counts[:, None]
    number = jnp.arange(steps * slots, dtype=jnp.int32).reshape(steps, slots)
    hit = (key[:, None, :] == jnp.arange(RT * RT, dtype=jnp.int32)[None, :, None]) & live[:, None, :]
    found = jnp.max(jnp.where(hit, number[:, None, :], -1), axis=2)
    return jnp.where(found < 0, steps * slots, found).reshape(-1)


def on_device(
    features, tile_weights, tile_rows, tile_cols, tile_counts, weight_self, weight_neigh, cotangent
):
    table = slot_table(tile_rows[0, 0], tile_cols[0, 0], tile_counts[0, 0])
    weights = tile_weights.reshape(STEPS * SLOTS, TILE, TILE)
    vmem = pl.BlockSpec(memory_space=pltpu.VMEM)
    dma = pltpu.SemaphoreType.DMA
    output, self_term, neigh_term = pl.pallas_call(
        aggregate_kernel,
        out_shape=(
            jax.ShapeDtypeStruct((QUARTER, WIDTH), jnp.bfloat16),
            jax.ShapeDtypeStruct((WIDTH, WIDTH), jnp.float32),
            jax.ShapeDtypeStruct((WIDTH, WIDTH), jnp.float32),
        ),
        in_specs=[
            pl.BlockSpec(memory_space=pltpu.SMEM),
            vmem,
            pl.BlockSpec(memory_space=pl.ANY),
            vmem,
            vmem,
            vmem,
        ],
        out_specs=(vmem, vmem, vmem),
        scratch_shapes=[
            pltpu.VMEM((STEPS * SLOTS + 1, TILE, TILE), jnp.bfloat16),
            pltpu.VMEM((2 * STEPS, SUBS, SUB, WIDTH), jnp.bfloat16),
            pltpu.VMEM((STEPS, SUBS, SUB, WIDTH), jnp.bfloat16),
            pltpu.VMEM((ROWS, WIDTH), jnp.float32),
            pltpu.VMEM((2, QUARTER, WIDTH), jnp.float32),
            pltpu.VMEM((2, QUARTER, WIDTH), jnp.float32),
            pltpu.VMEM((QUARTER, WIDTH), jnp.bfloat16),
            pltpu.VMEM((QUARTER, WIDTH), jnp.bfloat16),
            dma((STEPS,)),
            dma((1,)),
            dma((2 * STEPS, SUBS)),
            dma((STEPS,)),
            dma((2,)),
            dma,
            dma((SUBS,)),
            dma((2, SUBS)),
            dma((SUBS,)),
            dma((4, 2)),
            dma((4, 2)),
            dma((4,)),
            dma((4,)),
            dma((2, 4)),
            dma((4,)),
            dma((STEPS,)),
            dma((2,)),
            dma,
        ],
        compiler_params=pltpu.CompilerParams(
            collective_id=0, has_side_effects=True, vmem_limit_bytes=60 * 1024 * 1024
        ),
    )(
        table,
        features.reshape(2, SUBS, SUB, WIDTH),
        weights,
        weight_self,
        weight_neigh,
        cotangent,
    )
    grad_self, grad_neigh = lax.psum((self_term, neigh_term), ("dom", "rep"))
    return (output, grad_self, grad_neigh)


def solution(mesh):
    return jax.shard_map(
        on_device,
        mesh=mesh,
        in_specs=(
            P("dom", None),
            P("dom", "rep", None, None, None, None),
            P("dom", "rep", None, None),
            P("dom", "rep", None, None),
            P("dom", "rep", None),
            P(),
            P(),
            P(("dom", "rep"), None),
        ),
        out_specs=(P(("dom", "rep"), None), P(), P()),
        check_vma=False,
    )
```

```python
import jax
import jax.numpy as jnp
from jax import lax
from jax.experimental import pallas as pl
from jax.experimental.pallas import tpu as pltpu
from jax.sharding import PartitionSpec as P

MESH = pl.DeviceIdType.MESH
BLOCKS = 32
STEPS = 8
SLOTS = 88
TILE = 128
RT = 12
WIDTH = 256
SUBS = 3
SUB = 256
ROWS = 1536
QUARTER = 384
CHIPS = 64


def where_am_i():
    p = lax.axis_index("dom")
    rep = lax.axis_index("rep")
    copy, core = rep // 2, rep % 2
    g = (p + 16 * copy) % BLOCKS
    return copy, core, g


def device(copy, g, core):
    return ((g + 16 * copy) % BLOCKS, 2 * copy + core)


def at(z, y):
    return (z % 8) * 4 + y


def aggregate_kernel(
    slots,
    features,
    weights,
    weight_self,
    weight_neigh,
    cotangent,
    out_ref,
    self_ref,
    neigh_ref,
    wbuf,
    fbuf,
    obuf,
    acc,
    r1buf,
    r1src,
    r2src,
    r2buf,
    w_sem,
    own_sem,
    f_sem,
    o_sem,
    r1_sem,
    r2_sem,
    s_swap,
    s_y,
    s_yr,
    s_zd,
    s_zu,
    s_rd,
    s_ru,
    s_x,
    s_x2,
    s_o,
    s_r1,
    s_r2,
    gsrc,
    gin,
    gsum,
    rsbuf,
    agbuf,
    agother,
    g0_sem,
    rs_sem,
    ag_sem,
    g1_sem,
    s_g0,
    s_rs,
    s_ag,
    s_g1,
):
    k, c, g = where_am_i()
    z, y = g // 4, g % 4
    first, mine_no = k, 1 - k

    other_core = device(k, g, 1 - c)
    other_copy = device(1 - k, g, c)
    y_up, y_down = (y + 1) % 4, (y + 3) % 4
    to_y_up = device(k, at(z, y_up), c)
    to_y_down = device(k, at(z, y_down), c)
    to_z_down = device(k, at(z + 7, y), c)
    to_z_up = device(k, at(z + 1, y), c)
    to_z_flip = device(k, at(z + 5, y), c)
    to_z_flip_back = device(k, at(z + 3, y), c)
    to_twin = device(k, (g + 16) % BLOCKS, c)
    to_rep = device(1 - k, (g + 16) % BLOCKS, c)

    for step in range(STEPS):
        pltpu.make_async_copy(
            weights.at[pl.ds(step * SLOTS, SLOTS)], wbuf.at[pl.ds(step * SLOTS, SLOTS)], w_sem.at[step]
        ).start()

    barrier = pltpu.get_barrier_semaphore()
    partners = (
        other_core,
        other_copy,
        to_y_up,
        to_y_down,
        to_z_down,
        to_z_up,
        to_z_flip,
        to_z_flip_back,
        to_twin,
        to_rep,
    )
    for partner in partners:
        pl.semaphore_signal(barrier, inc=1, device_id=partner, device_id_type=MESH)
    wbuf[STEPS * SLOTS] = jnp.zeros((TILE, TILE), wbuf.dtype)
    pl.semaphore_wait(barrier, len(partners))

    def push(slot_from, sub_from, slot_to, send_sem, target):
        pltpu.make_async_remote_copy(
            src_ref=fbuf.at[slot_from, sub_from],
            dst_ref=fbuf.at[slot_to, sub_from],
            send_sem=send_sem,
            recv_sem=f_sem.at[slot_to, sub_from],
            device_id=target,
            device_id_type=MESH,
        ).start()

    def arrived(slot, sub):
        pltpu.make_async_copy(fbuf.at[slot, sub], fbuf.at[slot, sub], f_sem.at[slot, sub]).wait()

    def sent(sem):
        pltpu.make_async_copy(fbuf.at[0, 0], fbuf.at[0, 0], sem).wait()

    def give_core(slot):
        pltpu.make_async_remote_copy(
            src_ref=fbuf.at[slot],
            dst_ref=obuf.at[slot % STEPS],
            send_sem=s_o.at[slot % STEPS],
            recv_sem=o_sem.at[slot % STEPS],
            device_id=other_core,
            device_id_type=MESH,
        ).start()

    def swap(sub, target):
        pltpu.make_async_remote_copy(
            src_ref=features.at[c, sub],
            dst_ref=fbuf.at[4, sub],
            send_sem=s_swap.at[sub],
            recv_sem=f_sem.at[4, sub],
            device_id=target,
            device_id_type=MESH,
        ).start()

    sender = jnp.logical_or(jnp.logical_and(k == 0, c == 0), jnp.logical_and(k == 1, c == 1))

    @pl.when(jnp.logical_and(k == 0, c == 0))
    def _():
        for sub in range(SUBS):
            swap(sub, other_copy)

    @pl.when(jnp.logical_and(k == 1, c == 1))
    def _():
        for sub in range(SUBS):
            swap(sub, to_twin)

    @pl.when(k == 0)
    def _():
        for sub in range(SUBS):
            pltpu.make_async_copy(features.at[c, sub], fbuf.at[4, sub], f_sem.at[4, sub]).start()

    def z_sends(slot, block_y, j):
        delta = block_y - y
        for n, sub in enumerate((first, 2)):
            push(slot, sub, 8 + delta, s_zd.at[j, n], to_z_down)
        above = delta >= 0
        z_to = jnp.where(above, z + 1, z + 5)
        target = device(k, at(z_to, y), c)
        for n, sub in enumerate((first, 2)):
            push(slot, sub, (delta + 16) % 16, s_zu.at[j, n], target)

    for sub in range(SUBS):
        arrived(4, sub)
        push(4, sub, 4 + y - y_up, s_y.at[0, sub], to_y_up)
        push(4, sub, 4 + y - y_down, s_y.at[1, sub], to_y_down)
    z_sends(4, y, 0)

    @pl.when(c == 1)
    def _():
        give_core(4)

    from_up = 4 + y_up - y
    from_down = 4 + y_down - y
    for sub in range(SUBS):
        arrived(from_down, sub)
        if sub != 1:
            push(from_down, sub, 4 + y_down - y_up, s_yr.at[sub], to_y_up)
        arrived(from_up, sub)
        if sub == 1:
            push(from_up, sub, 4 + y_up - y_down, s_yr.at[sub], to_y_down)
    z_sends(from_up, y_up, 1)
    z_sends(from_down, y_down, 3)

    @pl.when(c == 1)
    def _():
        give_core(from_up)
        give_core(from_down)

    opposite = (y + 2) % 4
    from_opposite = 4 + opposite - y
    for sub in range(SUBS):
        arrived(from_opposite, sub)
    z_sends(from_opposite, opposite, 2)

    @pl.when(c == 1)
    def _():
        give_core(from_opposite)

    acc[...] = jnp.zeros_like(acc)
    for step in range(STEPS):
        pltpu.make_async_copy(
            weights.at[pl.ds(step * SLOTS, SLOTS)], wbuf.at[pl.ds(step * SLOTS, SLOTS)], w_sem.at[step]
        ).wait()

    group = 3

    def multiply(slot):
        step = slot % STEPS
        pltpu.make_async_copy(obuf.at[step], obuf.at[step], o_sem.at[step]).wait()
        half_cols = RT // 2

        def rows_of(r, carry):
            base = step * (RT * RT) + r * (group * RT)
            total = None
            for ref, at_slot, side in ((fbuf, slot, c), (obuf, step, 1 - c)):
                stacked = []
                for n in range(group):
                    tiles = [
                        wbuf[slots[base + n * RT + half_cols * side + i]] for i in range(half_cols)
                    ]
                    stacked.append(jnp.concatenate(tiles, axis=1))
                lhs = jnp.concatenate(stacked, axis=0)
                rhs = ref[at_slot].reshape(SUBS * SUB, WIDTH)
                term = jnp.dot(lhs, rhs, preferred_element_type=jnp.float32)
                total = term if total is None else total + term
            window = pl.ds(pl.multiple_of(r * (group * TILE), group * TILE), group * TILE)
            acc[window, :] += total
            return carry

        lax.fori_loop(0, RT // group, rows_of, 0)

    def order(i):
        return i + i // 2 - 2 * (i // 3)

    def delta_of(i):
        return (y + order(i)) % 4 - y

    def first_pass(i, carry):
        delta = delta_of(i)
        above = 8 + delta
        below = (delta + 16) % 16
        far = 12 + delta
        arrived(above, first)
        push(above, first, far, s_rd.at[i], to_z_down)
        push(above, first, above, s_x.at[0, i], other_copy)
        arrived(above, 2)
        arrived(below, first)
        push(below, first, below, s_x.at[1, i], other_copy)
        arrived(below, 2)
        z_to = jnp.where(delta >= 0, z + 5, z + 1)
        push(below, 2, far, s_ru.at[i], device(k, at(z_to, y), c))

        @pl.when(c == 0)
        def _():
            multiply(4 + delta)

        return carry

    lax.fori_loop(0, 4, first_pass, 0)

    def second_pass(i, carry):
        delta = delta_of(i)
        above = 8 + delta
        below = (delta + 16) % 16
        far = 12 + delta
        arrived(far, first)
        push(far, first, far, s_x2.at[i], other_copy)
        arrived(above, mine_no)
        arrived(below, mine_no)
        mine = jnp.where(above // STEPS == c, above, below)
        theirs = above + below - mine
        give_core(theirs)
        multiply(mine)
        return carry

    lax.fori_loop(0, 4, second_pass, 0)

    def third_pass(i, carry):
        far = 12 + delta_of(i)
        arrived(far, 2)
        arrived(far, mine_no)

        @pl.when(c == 0)
        def _():
            give_core(far)

        @pl.when(c == 1)
        def _():
            multiply(far)

        return carry

    lax.fori_loop(0, 4, third_pass, 0)

    for part in range(2):
        start = pl.multiple_of((2 * part + 1 - c) * QUARTER, QUARTER)
        r1src[part] = acc[pl.ds(start, QUARTER), :]
        pltpu.make_async_remote_copy(
            src_ref=r1src.at[part],
            dst_ref=r1buf.at[part],
            send_sem=s_r1.at[part],
            recv_sem=r1_sem.at[part],
            device_id=other_core,
            device_id_type=MESH,
        ).start()

    for sem in [s_y.at[d, s] for d in range(2) for s in range(SUBS)] + [s_yr.at[s] for s in range(SUBS)]:
        sent(sem)
    for j in range(4):
        for n in range(2):
            sent(s_zd.at[j, n])
            sent(s_zu.at[j, n])
            sent(s_x.at[n, j])
        sent(s_rd.at[j])
        sent(s_ru.at[j])
        sent(s_x2.at[j])
    for step in range(STEPS):
        pltpu.make_async_copy(obuf.at[step], obuf.at[step], s_o.at[step]).wait()

    @pl.when(sender)
    def _():
        for sub in range(SUBS):
            sent(s_swap.at[sub])

    for part in range(2):
        pltpu.make_async_copy(r1buf.at[part], r1buf.at[part], r1_sem.at[part]).wait()

    away = pl.multiple_of((2 * (1 - k) + c) * QUARTER, QUARTER)
    r2src[...] = (acc[pl.ds(away, QUARTER), :] + r1buf[1 - k]).astype(r2src.dtype)
    cross = pltpu.make_async_remote_copy(
        src_ref=r2src,
        dst_ref=r2buf,
        send_sem=s_r2,
        recv_sem=r2_sem,
        device_id=to_rep,
        device_id_type=MESH,
    )
    cross.start()
    home = pl.multiple_of((2 * k + c) * QUARTER, QUARTER)
    kept = acc[pl.ds(home, QUARTER), :] + r1buf[k]
    own = features.reshape(ROWS, WIDTH)[pl.ds(home, QUARTER), :]
    pre = jnp.dot(own, weight_self[...], preferred_element_type=jnp.float32)
    cross.wait()
    aggregate = (kept + r2buf[...].astype(jnp.float32)).astype(jnp.bfloat16)
    pre = pre + jnp.dot(aggregate, weight_neigh[...], preferred_element_type=jnp.float32)
    sigmoid = jax.nn.sigmoid(pre)
    out_ref[...] = (pre * sigmoid).astype(out_ref.dtype)
    slope = (cotangent[...].astype(jnp.float32) * sigmoid * (1.0 + pre * (1.0 - sigmoid))).astype(
        jnp.bfloat16
    )
    contract = (((0,), (0,)), ((), ()))
    self_term = lax.dot_general(own, slope, contract, preferred_element_type=jnp.float32)
    neigh_term = lax.dot_general(aggregate, slope, contract, preferred_element_type=jnp.float32)
    gsrc[...] = jnp.where(c == 0, neigh_term, self_term)
    core_swap = pltpu.make_async_remote_copy(
        src_ref=gsrc,
        dst_ref=gin,
        send_sem=s_g0,
        recv_sem=g0_sem,
        device_id=other_core,
        device_id_type=MESH,
    )
    core_swap.start()
    for part in range(2):
        pltpu.make_async_copy(r1src.at[part], r1src.at[part], s_r1.at[part]).wait()
    core_swap.wait()
    chip_term = jnp.where(c == 0, self_term, neigh_term) + gin[...]
    for side in range(2):
        gsum[:, side] = chip_term[:, side * TILE : (side + 1) * TILE].reshape(CHIPS // 2, 8, TILE)
    me = 32 * k + g

    def scatter(t, carry):
        peer = (me + t) % CHIPS
        pltpu.make_async_remote_copy(
            src_ref=gsum.at[peer // 2, peer % 2],
            dst_ref=rsbuf.at[t - 1],
            send_sem=s_rs,
            recv_sem=rs_sem,
            device_id=device(peer // 32, peer % 32, c),
            device_id_type=MESH,
        ).start()
        return carry

    lax.fori_loop(1, CHIPS, scatter, 0)
    everything = pltpu.make_async_copy(rsbuf, rsbuf, rs_sem)
    everything.wait()
    piece = gsum[me // 2, me % 2] + jnp.sum(rsbuf[...], axis=0)
    agbuf[me // 2, me % 2] = piece

    def gather(t, carry):
        peer = (me + t) % CHIPS
        pltpu.make_async_remote_copy(
            src_ref=agbuf.at[me // 2, me % 2],
            dst_ref=agbuf.at[me // 2, me % 2],
            send_sem=s_ag,
            recv_sem=ag_sem,
            device_id=device(peer // 32, peer % 32, c),
            device_id_type=MESH,
        ).start()
        return carry

    lax.fori_loop(1, CHIPS, gather, 0)
    pltpu.make_async_copy(rsbuf, rsbuf, s_rs).wait()
    pltpu.make_async_copy(rsbuf, rsbuf, ag_sem).wait()
    last = pltpu.make_async_remote_copy(
        src_ref=agbuf,
        dst_ref=agother,
        send_sem=s_g1,
        recv_sem=g1_sem,
        device_id=other_core,
        device_id_type=MESH,
    )
    last.start()
    pltpu.make_async_copy(rsbuf, rsbuf, s_ag).wait()
    last.wait()
    for side in range(2):
        lanes = slice(side * TILE, (side + 1) * TILE)
        held = agbuf[:, side].reshape(WIDTH, TILE)
        came = agother[:, side].reshape(WIDTH, TILE)
        self_ref[:, lanes] = jnp.where(c == 0, held, came)
        neigh_ref[:, lanes] = jnp.where(c == 0, came, held)


def slot_table(rows, cols, counts):
    steps, slots = rows.shape
    key = rows * RT + cols
    live = jnp.arange(slots, dtype=jnp.int32)[None, :] < counts[:, None]
    number = jnp.arange(steps * slots, dtype=jnp.int32).reshape(steps, slots)
    hit = (key[:, None, :] == jnp.arange(RT * RT, dtype=jnp.int32)[None, :, None]) & live[:, None, :]
    found = jnp.max(jnp.where(hit, number[:, None, :], -1), axis=2)
    return jnp.where(found < 0, steps * slots, found).reshape(-1)


def on_device(
    features, tile_weights, tile_rows, tile_cols, tile_counts, weight_self, weight_neigh, cotangent
):
    table = slot_table(tile_rows[0, 0], tile_cols[0, 0], tile_counts[0, 0])
    weights = tile_weights.reshape(STEPS * SLOTS, TILE, TILE)
    vmem = pl.BlockSpec(memory_space=pltpu.VMEM)
    dma = pltpu.SemaphoreType.DMA
    return pl.pallas_call(
        aggregate_kernel,
        out_shape=(
            jax.ShapeDtypeStruct((QUARTER, WIDTH), jnp.bfloat16),
            jax.ShapeDtypeStruct((WIDTH, WIDTH), jnp.float32),
            jax.ShapeDtypeStruct((WIDTH, WIDTH), jnp.float32),
        ),
        in_specs=[
            pl.BlockSpec(memory_space=pltpu.SMEM),
            vmem,
            pl.BlockSpec(memory_space=pl.ANY),
            vmem,
            vmem,
            vmem,
        ],
        out_specs=(vmem, vmem, vmem),
        scratch_shapes=[
            pltpu.VMEM((STEPS * SLOTS + 1, TILE, TILE), jnp.bfloat16),
            pltpu.VMEM((2 * STEPS, SUBS, SUB, WIDTH), jnp.bfloat16),
            pltpu.VMEM((STEPS, SUBS, SUB, WIDTH), jnp.bfloat16),
            pltpu.VMEM((ROWS, WIDTH), jnp.float32),
            pltpu.VMEM((2, QUARTER, WIDTH), jnp.float32),
            pltpu.VMEM((2, QUARTER, WIDTH), jnp.float32),
            pltpu.VMEM((QUARTER, WIDTH), jnp.bfloat16),
            pltpu.VMEM((QUARTER, WIDTH), jnp.bfloat16),
            dma((STEPS,)),
            dma((1,)),
            dma((2 * STEPS, SUBS)),
            dma((STEPS,)),
            dma((2,)),
            dma,
            dma((SUBS,)),
            dma((2, SUBS)),
            dma((SUBS,)),
            dma((4, 2)),
            dma((4, 2)),
            dma((4,)),
            dma((4,)),
            dma((2, 4)),
            dma((4,)),
            dma((STEPS,)),
            dma((2,)),
            dma,
            pltpu.VMEM((WIDTH, WIDTH), jnp.float32),
            pltpu.VMEM((WIDTH, WIDTH), jnp.float32),
            pltpu.VMEM((CHIPS // 2, 2, 8, TILE), jnp.float32),
            pltpu.VMEM((CHIPS - 1, 8, TILE), jnp.float32),
            pltpu.VMEM((CHIPS // 2, 2, 8, TILE), jnp.float32),
            pltpu.VMEM((CHIPS // 2, 2, 8, TILE), jnp.float32),
            dma,
            dma,
            dma,
            dma,
            dma,
            dma,
            dma,
            dma,
        ],
        compiler_params=pltpu.CompilerParams(
            collective_id=0, has_side_effects=True, vmem_limit_bytes=60 * 1024 * 1024
        ),
    )(
        table,
        features.reshape(2, SUBS, SUB, WIDTH),
        weights,
        weight_self,
        weight_neigh,
        cotangent,
    )


def solution(mesh):
    return jax.shard_map(
        on_device,
        mesh=mesh,
        in_specs=(
            P("dom", None),
            P("dom", "rep", None, None, None, None),
            P("dom", "rep", None, None),
            P("dom", "rep", None, None),
            P("dom", "rep", None),
            P(),
            P(),
            P(("dom", "rep"), None),
        ),
        out_specs=(P(("dom", "rep"), None), P(), P()),
        check_vma=False,
    )
```

```python
import jax
import jax.numpy as jnp
from jax import lax
from jax.experimental import pallas as pl
from jax.experimental.pallas import tpu as pltpu
from jax.sharding import PartitionSpec as P

MESH = pl.DeviceIdType.MESH
BLOCKS = 32
STEPS = 8
SLOTS = 88
TILE = 128
RT = 12
WIDTH = 256
EDGE = 192
COMMON = 384
HALF = 768
ROWS = 1536
QUARTER = 384
CHIPS = 64


def where_am_i():
    p = lax.axis_index("dom")
    rep = lax.axis_index("rep")
    copy, core = rep // 2, rep % 2
    g = (p + 16 * copy) % BLOCKS
    return copy, core, g


def device(copy, g, core):
    return ((g + 16 * copy) % BLOCKS, 2 * copy + core)


def at(z, y):
    return (z % 8) * 4 + y


def aggregate_kernel(
    slots,
    features,
    weights,
    weight_self,
    weight_neigh,
    cotangent,
    out_ref,
    self_ref,
    neigh_ref,
    wbuf,
    fbuf,
    obuf,
    acc,
    r1buf,
    r2src,
    r2buf,
    w_sem,
    own_sem,
    f_sem,
    o_sem,
    r1_sem,
    r2_sem,
    s_swap,
    s_y,
    s_yr,
    s_zd,
    s_zu,
    s_rd,
    s_ru,
    s_x,
    s_x2,
    s_o,
    s_r1,
    s_r2,
    gsrc,
    gin,
    gsum,
    rsbuf,
    agbuf,
    agother,
    g0_sem,
    rs_sem,
    ag_sem,
    g1_sem,
    s_g0,
    s_rs,
    s_ag,
    s_g1,
    tbuf,
    t_sem,
    s_t,
    s_fy,
    s_fyr,
):
    k, c, g = where_am_i()
    z, y = g // 4, g % 4
    first, mine_no = k, 1 - k

    other_core = device(k, g, 1 - c)
    other_copy = device(1 - k, g, c)
    y_up, y_down = (y + 1) % 4, (y + 3) % 4
    to_y_up = device(k, at(z, y_up), c)
    to_y_down = device(k, at(z, y_down), c)
    to_z_down = device(k, at(z + 7, y), c)
    to_z_up = device(k, at(z + 1, y), c)
    to_z_flip = device(k, at(z + 5, y), c)
    to_z_flip_back = device(k, at(z + 3, y), c)
    to_twin = device(k, (g + 16) % BLOCKS, c)
    to_rep = device(1 - k, (g + 16) % BLOCKS, c)

    for step in range(STEPS):
        pltpu.make_async_copy(
            weights.at[pl.ds(step * SLOTS, SLOTS)], wbuf.at[pl.ds(step * SLOTS, SLOTS)], w_sem.at[step]
        ).start()

    barrier = pltpu.get_barrier_semaphore()
    partners = (
        other_core,
        other_copy,
        to_y_up,
        to_y_down,
        to_z_down,
        to_z_up,
        to_z_flip,
        to_z_flip_back,
        to_twin,
        to_rep,
    )
    for partner in partners:
        pl.semaphore_signal(barrier, inc=1, device_id=partner, device_id_type=MESH)
    wbuf[STEPS * SLOTS] = jnp.zeros((TILE, TILE), wbuf.dtype)
    pl.semaphore_wait(barrier, len(partners))

    subs = ((first, EDGE * k, EDGE), (2, 2 * EDGE, COMMON), (mine_no, EDGE * (1 - k), EDGE))

    def part_of(ref, n):
        _, start, size = subs[n]
        return ref.at[pl.ds(pl.multiple_of(start, EDGE), size)]

    def push(slot_from, n, slot_to, send_sem, target):
        pltpu.make_async_remote_copy(
            src_ref=part_of(fbuf.at[slot_from], n),
            dst_ref=part_of(fbuf.at[slot_to], n),
            send_sem=send_sem,
            recv_sem=f_sem.at[slot_to, subs[n][0]],
            device_id=target,
            device_id_type=MESH,
        ).start()

    def arrived(slot, n):
        here = part_of(fbuf.at[slot], n)
        pltpu.make_async_copy(here, here, f_sem.at[slot, subs[n][0]]).wait()

    def sent(sem, n):
        here = part_of(fbuf.at[0], n)
        pltpu.make_async_copy(here, here, sem).wait()

    def give_core(slot):
        pltpu.make_async_remote_copy(
            src_ref=fbuf.at[slot],
            dst_ref=obuf.at[slot % STEPS],
            send_sem=s_o.at[slot % STEPS],
            recv_sem=o_sem.at[slot % STEPS],
            device_id=other_core,
            device_id_type=MESH,
        ).start()

    cuts = ((0, 0, EDGE), (1, EDGE, EDGE), (2, 2 * EDGE, COMMON))

    def swap(target):
        for number, start, size in cuts:
            pltpu.make_async_remote_copy(
                src_ref=features.at[c, pl.ds(start, size)],
                dst_ref=fbuf.at[4, pl.ds(start, size)],
                send_sem=s_swap.at[number],
                recv_sem=f_sem.at[4, number],
                device_id=target,
                device_id_type=MESH,
            ).start()

    sender = jnp.logical_or(jnp.logical_and(k == 0, c == 0), jnp.logical_and(k == 1, c == 1))

    @pl.when(jnp.logical_and(k == 0, c == 0))
    def _():
        swap(other_copy)

    @pl.when(jnp.logical_and(k == 1, c == 1))
    def _():
        swap(to_twin)

    @pl.when(k == 0)
    def _():
        for number, start, size in cuts:
            pltpu.make_async_copy(
                features.at[c, pl.ds(start, size)], fbuf.at[4, pl.ds(start, size)], f_sem.at[4, number]
            ).start()

    edge_low = z % 4 == 0
    edge_high = z % 4 == 3
    to_plane = device(k, at(z + 3, y), c)

    def turns(edge, delta, j, n):
        if n == 0:
            return jnp.logical_and(edge, j != 0)
        return jnp.logical_and(edge, delta < 0)

    def z_sends(slot, block_y, j, n):
        delta = block_y - y
        turn = turns(edge_low, delta, j, n)

        @pl.when(turn)
        def _():
            pltpu.make_async_remote_copy(
                src_ref=part_of(fbuf.at[slot], n),
                dst_ref=part_of(tbuf.at[j], n),
                send_sem=s_zd.at[j, n],
                recv_sem=t_sem.at[j, n],
                device_id=to_plane,
                device_id_type=MESH,
            ).start()

        @pl.when(jnp.logical_not(turn))
        def _():
            push(slot, n, 8 + delta, s_zd.at[j, n], to_z_down)

        z_to = jnp.where(delta >= 0, z + 1, z + 5)
        target = device(k, at(z_to, y), c)
        push(slot, n, (delta + 16) % 16, s_zu.at[j, n], target)

    def turn_corner(delta, j, n):
        @pl.when(turns(edge_high, delta, j, n))
        def _():
            here = part_of(tbuf.at[j], n)
            pltpu.make_async_copy(here, here, t_sem.at[j, n]).wait()
            pltpu.make_async_remote_copy(
                src_ref=here,
                dst_ref=part_of(fbuf.at[8 + delta], n),
                send_sem=s_t.at[j, n],
                recv_sem=f_sem.at[8 + delta, subs[n][0]],
                device_id=to_twin,
                device_id_type=MESH,
            ).start()

    def share(slot, sem):
        push(slot, 0, slot, sem, other_copy)

    def share_edge(delta, i):
        above = 8 + delta
        below = (delta + 16) % 16
        arrived(below, 0)
        share(below, s_x.at[1, i])
        arrived(above, 0)
        share(above, s_x.at[0, i])

    for n in range(3):
        arrived(4, n)
        push(4, n, 4 + y - y_up, s_y.at[0, n], to_y_up)
        push(4, n, 4 + y - y_down, s_y.at[1, n], to_y_down)
        if n < 2:
            z_sends(4, y, 0, n)

    @pl.when(c == 1)
    def _():
        give_core(4)

    from_up = 4 + y_up - y
    from_down = 4 + y_down - y
    for n in range(3):
        if n == 0:
            arrived(8, 0)
            push(8, 0, 12, s_rd, to_z_down)
        if n == 1:
            arrived(0, 1)
            push(0, 1, 12, s_ru, device(k, at(z + 5, y), c))
        arrived(from_down, n)
        if n != 1:
            push(from_down, n, 4 + y_down - y_up, s_yr.at[n], to_y_up)
        if n == 0:
            z_sends(from_down, y_down, 3, n)
        arrived(from_up, n)
        if n == 1:
            push(from_up, n, 4 + y_up - y_down, s_yr.at[n], to_y_down)
        if n == 0:
            z_sends(from_up, y_up, 1, n)
        if n == 0:
            share(8, s_x.at[0, 0])
            arrived(0, 0)
            share(0, s_x.at[1, 0])

    @pl.when(c == 1)
    def _():
        give_core(from_up)
        give_core(from_down)

    opposite = (y + 2) % 4
    from_opposite = 4 + opposite - y
    arrived(from_opposite, 0)
    z_sends(from_opposite, opposite, 2, 0)
    z_sends(from_down, y_down, 3, 1)
    z_sends(from_up, y_up, 1, 1)
    arrived(from_opposite, 1)
    z_sends(from_opposite, opposite, 2, 1)
    arrived(from_opposite, 2)

    @pl.when(c == 1)
    def _():
        give_core(from_opposite)

    far_up = 12 + y_up - y
    far_down = 12 + y_down - y
    far_opposite = 12 + opposite - y

    def far_spread(n):
        arrived(12, n)
        push(12, n, 12 + y - y_up, s_fy.at[0, n], to_y_up)
        push(12, n, 12 + y - y_down, s_fy.at[1, n], to_y_down)

    far_spread(0)
    share(12, s_x2.at[0])
    turn_corner(y_up - y, 1, 0)
    turn_corner(y_down - y, 3, 0)
    share_edge(y_up - y, 1)
    share_edge(y_down - y, 3)

    acc[...] = jnp.zeros_like(acc)
    for step in range(STEPS):
        pltpu.make_async_copy(
            weights.at[pl.ds(step * SLOTS, SLOTS)], wbuf.at[pl.ds(step * SLOTS, SLOTS)], w_sem.at[step]
        ).wait()

    group = 6

    def multiply(slot):
        step = slot % STEPS
        pltpu.make_async_copy(obuf.at[step], obuf.at[step], o_sem.at[step]).wait()
        half_cols = RT // 2

        def rows_of(r, carry):
            base = step * (RT * RT) + r * (group * RT)
            total = None
            for ref, at_slot, side in ((fbuf, slot, c), (obuf, step, 1 - c)):
                stacked = []
                for n in range(group):
                    tiles = [
                        wbuf[slots[base + n * RT + half_cols * side + i]] for i in range(half_cols)
                    ]
                    stacked.append(jnp.concatenate(tiles, axis=1))
                lhs = jnp.concatenate(stacked, axis=0)
                term = jnp.dot(lhs, ref[at_slot], preferred_element_type=jnp.float32)
                total = term if total is None else total + term
            window = pl.ds(pl.multiple_of(r * (group * TILE), group * TILE), group * TILE)
            acc[window, :] += total
            return carry

        lax.fori_loop(0, RT // group, rows_of, 0)

    def order(i):
        return i + i // 2 - 2 * (i // 3)

    def delta_of(i):
        return (y + order(i)) % 4 - y

    def early_pass(i, carry):
        multiply(4 + delta_of(i))
        return carry

    def far_pass(i, carry):
        far = 12 + delta_of(i)
        arrived(far, 2)

        @pl.when(c == 0)
        def _():
            give_core(far)

        @pl.when(c == 1)
        def _():
            multiply(far)

        return carry

    def late_pass(i, carry):
        delta = delta_of(i)
        above = 8 + delta
        below = (delta + 16) % 16

        @pl.when(i > 0)
        def _():
            arrived(below, 1)

        arrived(above, 1)
        arrived(above, 2)
        arrived(below, 2)
        mine = jnp.where(above // STEPS == c, above, below)
        theirs = above + below - mine
        give_core(theirs)
        multiply(mine)
        return carry

    far_spread(1)
    arrived(far_down, 0)
    push(far_down, 0, 12 + y_down - y_up, s_fyr.at[0], to_y_up)
    share(far_down, s_x2.at[3])
    arrived(far_up, 0)
    share(far_up, s_x2.at[1])
    turn_corner(opposite - y, 2, 0)
    share_edge(opposite - y, 2)

    @pl.when(c == 0)
    def _():
        lax.fori_loop(0, 2, early_pass, 0)

    turn_corner(y_up - y, 1, 1)
    turn_corner(y_down - y, 3, 1)
    arrived(far_up, 1)
    push(far_up, 1, 12 + y_up - y_down, s_fyr.at[1], to_y_down)
    arrived(far_opposite, 0)
    share(far_opposite, s_x2.at[2])

    @pl.when(c == 0)
    def _():
        lax.fori_loop(2, 4, early_pass, 0)

    lax.fori_loop(0, 1, late_pass, 0)
    turn_corner(opposite - y, 2, 1)
    lax.fori_loop(0, 1, far_pass, 0)
    arrived(far_down, 1)
    lax.fori_loop(1, 2, late_pass, 0)
    arrived(far_opposite, 1)
    lax.fori_loop(1, 4, far_pass, 0)
    lax.fori_loop(2, 4, late_pass, 0)

    for part in (1 - k, k):
        start = pl.multiple_of((2 * part + 1 - c) * QUARTER, QUARTER)
        pltpu.make_async_remote_copy(
            src_ref=acc.at[pl.ds(start, QUARTER)],
            dst_ref=r1buf.at[part],
            send_sem=s_r1.at[part],
            recv_sem=r1_sem.at[part],
            device_id=other_core,
            device_id_type=MESH,
        ).start()

    def r1_arrived(part):
        pltpu.make_async_copy(r1buf.at[part], r1buf.at[part], r1_sem.at[part]).wait()

    away = pl.multiple_of((2 * (1 - k) + c) * QUARTER, QUARTER)
    r1_arrived(1 - k)
    r2src[...] = (acc[pl.ds(away, QUARTER), :] + r1buf[1 - k]).astype(r2src.dtype)
    cross = pltpu.make_async_remote_copy(
        src_ref=r2src,
        dst_ref=r2buf,
        send_sem=s_r2,
        recv_sem=r2_sem,
        device_id=to_rep,
        device_id_type=MESH,
    )
    cross.start()
    r1_arrived(k)
    home = pl.multiple_of((2 * k + c) * QUARTER, QUARTER)
    kept = acc[pl.ds(home, QUARTER), :] + r1buf[k]
    own = features.reshape(ROWS, WIDTH)[pl.ds(home, QUARTER), :]
    pre = jnp.dot(own, weight_self[...], preferred_element_type=jnp.float32)
    cross.wait()
    aggregate = (kept + r2buf[...].astype(jnp.float32)).astype(jnp.bfloat16)
    pre = pre + jnp.dot(aggregate, weight_neigh[...], preferred_element_type=jnp.float32)
    sigmoid = jax.nn.sigmoid(pre)
    out_ref[...] = (pre * sigmoid).astype(out_ref.dtype)
    slope = (cotangent[...].astype(jnp.float32) * sigmoid * (1.0 + pre * (1.0 - sigmoid))).astype(
        jnp.bfloat16
    )
    contract = (((0,), (0,)), ((), ()))
    self_term = lax.dot_general(own, slope, contract, preferred_element_type=jnp.float32)
    neigh_term = lax.dot_general(aggregate, slope, contract, preferred_element_type=jnp.float32)
    gsrc[...] = jnp.where(c == 0, neigh_term, self_term)
    core_swap = pltpu.make_async_remote_copy(
        src_ref=gsrc,
        dst_ref=gin,
        send_sem=s_g0,
        recv_sem=g0_sem,
        device_id=other_core,
        device_id_type=MESH,
    )
    core_swap.start()
    for part in range(2):
        pltpu.make_async_copy(r1buf.at[part], r1buf.at[part], s_r1.at[part]).wait()
    core_swap.wait()
    chip_term = jnp.where(c == 0, self_term, neigh_term) + gin[...]
    for side in range(2):
        gsum[:, side] = chip_term[:, side * TILE : (side + 1) * TILE].reshape(CHIPS // 2, 8, TILE)
    me = 32 * k + g

    def scatter(t, carry):
        peer = (me + t) % CHIPS
        pltpu.make_async_remote_copy(
            src_ref=gsum.at[peer // 2, peer % 2],
            dst_ref=rsbuf.at[t - 1],
            send_sem=s_rs,
            recv_sem=rs_sem,
            device_id=device(peer // 32, peer % 32, c),
            device_id_type=MESH,
        ).start()
        return carry

    lax.fori_loop(1, CHIPS, scatter, 0)
    everything = pltpu.make_async_copy(rsbuf, rsbuf, rs_sem)
    everything.wait()
    piece = gsum[me // 2, me % 2] + jnp.sum(rsbuf[...], axis=0)
    agbuf[me // 2, me % 2] = piece.astype(agbuf.dtype)

    def gather(t, carry):
        peer = (me + t) % CHIPS
        pltpu.make_async_remote_copy(
            src_ref=agbuf.at[me // 2, me % 2],
            dst_ref=agbuf.at[me // 2, me % 2],
            send_sem=s_ag,
            recv_sem=ag_sem,
            device_id=device(peer // 32, peer % 32, c),
            device_id_type=MESH,
        ).start()
        return carry

    lax.fori_loop(1, CHIPS, gather, 0)

    for n in range(3):
        sent(s_y.at[0, n], n)
        sent(s_y.at[1, n], n)
        sent(s_yr.at[n], n)
    for j in range(4):
        for n in range(2):
            sent(s_zd.at[j, n], n)
            sent(s_zu.at[j, n], n)

            @pl.when(turns(edge_high, (y + j) % 4 - y, j, n))
            def _():
                sent(s_t.at[j, n], n)

            sent(s_x.at[n, j], 0)
        sent(s_x2.at[j], 0)
    sent(s_rd, 0)
    sent(s_ru, 1)
    for n in range(2):
        sent(s_fy.at[0, n], n)
        sent(s_fy.at[1, n], n)
        sent(s_fyr.at[n], n)
    for step in range(STEPS):
        pltpu.make_async_copy(obuf.at[step], obuf.at[step], s_o.at[step]).wait()

    @pl.when(sender)
    def _():
        for number, start, size in cuts:
            here = fbuf.at[4, pl.ds(start, size)]
            pltpu.make_async_copy(here, here, s_swap.at[number]).wait()

    pltpu.make_async_copy(rsbuf, rsbuf, s_rs).wait()
    came_in = agbuf.reshape(CHIPS, 8, TILE).at[pl.ds(0, CHIPS - 1)]
    pltpu.make_async_copy(came_in, came_in, ag_sem).wait()
    last = pltpu.make_async_remote_copy(
        src_ref=agbuf,
        dst_ref=agother,
        send_sem=s_g1,
        recv_sem=g1_sem,
        device_id=other_core,
        device_id_type=MESH,
    )
    last.start()
    pltpu.make_async_copy(came_in, came_in, s_ag).wait()
    last.wait()
    held = agbuf[...].astype(jnp.float32)
    came = agother[...].astype(jnp.float32)
    self_ref[...] = jnp.where(c == 0, held, came)
    neigh_ref[...] = jnp.where(c == 0, came, held)


def finish_kernel(out_in, self_in, neigh_in, out_ref, self_ref, neigh_ref):
    out_ref[...] = out_in[...]
    for side in range(2):
        lanes = slice(side * TILE, (side + 1) * TILE)
        self_ref[:, lanes] = self_in[:, side].reshape(WIDTH, TILE)
        neigh_ref[:, lanes] = neigh_in[:, side].reshape(WIDTH, TILE)


def slot_table(rows, cols, counts):
    steps, slots = rows.shape
    key = rows * RT + cols
    live = jnp.arange(slots, dtype=jnp.int32)[None, :] < counts[:, None]
    number = jnp.arange(steps * slots, dtype=jnp.int32).reshape(steps, slots)
    hit = (key[:, None, :] == jnp.arange(RT * RT, dtype=jnp.int32)[None, :, None]) & live[:, None, :]
    found = jnp.max(jnp.where(hit, number[:, None, :], -1), axis=2)
    return jnp.where(found < 0, steps * slots, found).reshape(-1)


def on_device(
    features, tile_weights, tile_rows, tile_cols, tile_counts, weight_self, weight_neigh, cotangent
):
    table = slot_table(tile_rows[0, 0], tile_cols[0, 0], tile_counts[0, 0])
    weights = tile_weights.reshape(STEPS * SLOTS, TILE, TILE)
    vmem = pl.BlockSpec(memory_space=pltpu.VMEM)
    dma = pltpu.SemaphoreType.DMA
    raw = pl.pallas_call(
        aggregate_kernel,
        out_shape=(
            jax.ShapeDtypeStruct((QUARTER, WIDTH), jnp.bfloat16),
            jax.ShapeDtypeStruct((CHIPS // 2, 2, 8, TILE), jnp.float32),
            jax.ShapeDtypeStruct((CHIPS // 2, 2, 8, TILE), jnp.float32),
        ),
        in_specs=[
            pl.BlockSpec(memory_space=pltpu.SMEM),
            vmem,
            pl.BlockSpec(memory_space=pl.ANY),
            vmem,
            vmem,
            vmem,
        ],
        out_specs=(vmem, vmem, vmem),
        scratch_shapes=[
            pltpu.VMEM((STEPS * SLOTS + 1, TILE, TILE), jnp.bfloat16),
            pltpu.VMEM((2 * STEPS, HALF, WIDTH), jnp.bfloat16),
            pltpu.VMEM((STEPS, HALF, WIDTH), jnp.bfloat16),
            pltpu.VMEM((ROWS, WIDTH), jnp.float32),
            pltpu.VMEM((2, QUARTER, WIDTH), jnp.float32),
            pltpu.VMEM((QUARTER, WIDTH), jnp.bfloat16),
            pltpu.VMEM((QUARTER, WIDTH), jnp.bfloat16),
            dma((STEPS,)),
            dma((1,)),
            dma((2 * STEPS, 3)),
            dma((STEPS,)),
            dma((2,)),
            dma,
            dma((3,)),
            dma((2, 3)),
            dma((3,)),
            dma((4, 2)),
            dma((4, 2)),
            dma,
            dma,
            dma((2, 4)),
            dma((4,)),
            dma((STEPS,)),
            dma((2,)),
            dma,
            pltpu.VMEM((WIDTH, WIDTH), jnp.float32),
            pltpu.VMEM((WIDTH, WIDTH), jnp.float32),
            pltpu.VMEM((CHIPS // 2, 2, 8, TILE), jnp.float32),
            pltpu.VMEM((CHIPS - 1, 8, TILE), jnp.float32),
            pltpu.VMEM((CHIPS // 2, 2, 8, TILE), jnp.bfloat16),
            pltpu.VMEM((CHIPS // 2, 2, 8, TILE), jnp.bfloat16),
            dma,
            dma,
            dma,
            dma,
            dma,
            dma,
            dma,
            dma,
            pltpu.VMEM((4, HALF, WIDTH), jnp.bfloat16),
            dma((4, 2)),
            dma((4, 2)),
            dma((2, 2)),
            dma((2,)),
        ],
        compiler_params=pltpu.CompilerParams(
            collective_id=0, has_side_effects=True, vmem_limit_bytes=60 * 1024 * 1024
        ),
    )(
        table,
        features.reshape(2, HALF, WIDTH),
        weights,
        weight_self,
        weight_neigh,
        cotangent,
    )
    return pl.pallas_call(
        finish_kernel,
        out_shape=(
            jax.ShapeDtypeStruct((QUARTER, WIDTH), jnp.bfloat16),
            jax.ShapeDtypeStruct((WIDTH, WIDTH), jnp.float32),
            jax.ShapeDtypeStruct((WIDTH, WIDTH), jnp.float32),
        ),
        in_specs=[vmem, vmem, vmem],
        out_specs=(vmem, vmem, vmem),
    )(*raw)


def solution(mesh):
    return jax.shard_map(
        on_device,
        mesh=mesh,
        in_specs=(
            P("dom", None),
            P("dom", "rep", None, None, None, None),
            P("dom", "rep", None, None),
            P("dom", "rep", None, None),
            P("dom", "rep", None),
            P(),
            P(),
            P(("dom", "rep"), None),
        ),
        out_specs=(P(("dom", "rep"), None), P(), P()),
        check_vma=False,
    )
```

```python
import jax
import jax.numpy as jnp
from jax import lax
from jax.experimental import pallas as pl
from jax.experimental.pallas import tpu as pltpu
from jax.sharding import PartitionSpec as P

MESH = pl.DeviceIdType.MESH
BLOCKS = 32
STEPS = 8
SLOTS = 88
TILE = 128
RT = 12
WIDTH = 256
EDGE = 192
COMMON = 384
HALF = 768
ROWS = 1536
QUARTER = 384
CHIPS = 64


def where_am_i():
    p = lax.axis_index("dom")
    rep = lax.axis_index("rep")
    copy, core = rep // 2, rep % 2
    g = (p + 16 * copy) % BLOCKS
    return copy, core, g


def device(copy, g, core):
    return ((g + 16 * copy) % BLOCKS, 2 * copy + core)


def at(z, y):
    return (z % 8) * 4 + y


def aggregate_kernel(
    counts,
    tile_rows,
    tile_cols,
    features,
    weights,
    weight_self,
    weight_neigh,
    cotangent,
    out_ref,
    self_ref,
    neigh_ref,
    wbuf,
    fbuf,
    obuf,
    acc,
    r1buf,
    r2src,
    r2buf,
    w_sem,
    own_sem,
    f_sem,
    o_sem,
    r1_sem,
    r2_sem,
    s_swap,
    s_y,
    s_yr,
    s_zd,
    s_zu,
    s_rd,
    s_ru,
    s_x,
    s_x2,
    s_o,
    s_r1,
    s_r2,
    gsrc,
    gin,
    gsum,
    rsbuf,
    agbuf,
    agother,
    g0_sem,
    rs_sem,
    ag_sem,
    g1_sem,
    s_g0,
    s_rs,
    s_ag,
    s_g1,
    tbuf,
    t_sem,
    s_t,
    s_fy,
    s_fyr,
    table,
    slots,
    table_sem,
):
    k, c, g = where_am_i()
    z, y = g // 4, g % 4
    first, mine_no = k, 1 - k

    other_core = device(k, g, 1 - c)
    other_copy = device(1 - k, g, c)
    y_up, y_down = (y + 1) % 4, (y + 3) % 4
    to_y_up = device(k, at(z, y_up), c)
    to_y_down = device(k, at(z, y_down), c)
    to_z_down = device(k, at(z + 7, y), c)
    to_z_up = device(k, at(z + 1, y), c)
    to_z_flip = device(k, at(z + 5, y), c)
    to_z_flip_back = device(k, at(z + 3, y), c)
    to_twin = device(k, (g + 16) % BLOCKS, c)
    to_rep = device(1 - k, (g + 16) % BLOCKS, c)

    for step in range(STEPS):
        pltpu.make_async_copy(
            weights.at[pl.ds(step * SLOTS, SLOTS)], wbuf.at[pl.ds(step * SLOTS, SLOTS)], w_sem.at[step]
        ).start()

    barrier = pltpu.get_barrier_semaphore()
    partners = (
        other_core,
        other_copy,
        to_y_up,
        to_y_down,
        to_z_down,
        to_z_up,
        to_z_flip,
        to_z_flip_back,
        to_twin,
        to_rep,
    )
    for partner in partners:
        pl.semaphore_signal(barrier, inc=1, device_id=partner, device_id_type=MESH)
    wbuf[STEPS * SLOTS] = jnp.zeros((TILE, TILE), wbuf.dtype)
    pl.semaphore_wait(barrier, len(partners))

    subs = ((first, EDGE * k, EDGE), (2, 2 * EDGE, COMMON), (mine_no, EDGE * (1 - k), EDGE))

    def part_of(ref, n):
        _, start, size = subs[n]
        return ref.at[pl.ds(pl.multiple_of(start, EDGE), size)]

    def push(slot_from, n, slot_to, send_sem, target):
        pltpu.make_async_remote_copy(
            src_ref=part_of(fbuf.at[slot_from], n),
            dst_ref=part_of(fbuf.at[slot_to], n),
            send_sem=send_sem,
            recv_sem=f_sem.at[slot_to, subs[n][0]],
            device_id=target,
            device_id_type=MESH,
        ).start()

    def arrived(slot, n):
        here = part_of(fbuf.at[slot], n)
        pltpu.make_async_copy(here, here, f_sem.at[slot, subs[n][0]]).wait()

    def sent(sem, n):
        here = part_of(fbuf.at[0], n)
        pltpu.make_async_copy(here, here, sem).wait()

    def give_core(slot):
        pltpu.make_async_remote_copy(
            src_ref=fbuf.at[slot],
            dst_ref=obuf.at[slot % STEPS],
            send_sem=s_o.at[slot % STEPS],
            recv_sem=o_sem.at[slot % STEPS],
            device_id=other_core,
            device_id_type=MESH,
        ).start()

    cuts = ((0, 0, EDGE), (1, EDGE, EDGE), (2, 2 * EDGE, COMMON))

    def swap(target):
        for number, start, size in (cuts[1], cuts[2], cuts[0]):
            pltpu.make_async_remote_copy(
                src_ref=features.at[c, pl.ds(start, size)],
                dst_ref=fbuf.at[4, pl.ds(start, size)],
                send_sem=s_swap.at[number],
                recv_sem=f_sem.at[4, number],
                device_id=target,
                device_id_type=MESH,
            ).start()

    sender = jnp.logical_or(jnp.logical_and(k == 0, c == 0), jnp.logical_and(k == 1, c == 1))

    @pl.when(jnp.logical_and(k == 0, c == 0))
    def _():
        swap(other_copy)

    @pl.when(jnp.logical_and(k == 1, c == 1))
    def _():
        swap(to_twin)

    @pl.when(k == 0)
    def _():
        for number, start, size in cuts:
            pltpu.make_async_copy(
                features.at[c, pl.ds(start, size)], fbuf.at[4, pl.ds(start, size)], f_sem.at[4, number]
            ).start()

    edge_low = z % 4 == 0
    edge_high = z % 4 == 3
    to_plane = device(k, at(z + 3, y), c)

    def turns(edge, delta, j, n):
        if n == 0:
            return jnp.logical_and(edge, j != 0)
        return jnp.logical_and(edge, delta < 0)

    def z_sends(slot, block_y, j, n):
        delta = block_y - y
        turn = turns(edge_low, delta, j, n)

        @pl.when(turn)
        def _():
            pltpu.make_async_remote_copy(
                src_ref=part_of(fbuf.at[slot], n),
                dst_ref=part_of(tbuf.at[j], n),
                send_sem=s_zd.at[j, n],
                recv_sem=t_sem.at[j, n],
                device_id=to_plane,
                device_id_type=MESH,
            ).start()

        @pl.when(jnp.logical_not(turn))
        def _():
            push(slot, n, 8 + delta, s_zd.at[j, n], to_z_down)

        z_to = jnp.where(delta >= 0, z + 1, z + 5)
        target = device(k, at(z_to, y), c)
        push(slot, n, (delta + 16) % 16, s_zu.at[j, n], target)

    def turn_corner(delta, j, n):
        @pl.when(turns(edge_high, delta, j, n))
        def _():
            here = part_of(tbuf.at[j], n)
            pltpu.make_async_copy(here, here, t_sem.at[j, n]).wait()
            pltpu.make_async_remote_copy(
                src_ref=here,
                dst_ref=part_of(fbuf.at[8 + delta], n),
                send_sem=s_t.at[j, n],
                recv_sem=f_sem.at[8 + delta, subs[n][0]],
                device_id=to_twin,
                device_id_type=MESH,
            ).start()

    def share(slot, sem):
        push(slot, 0, slot, sem, other_copy)

    def share_edge(delta, i):
        above = 8 + delta
        below = (delta + 16) % 16
        arrived(below, 0)
        share(below, s_x.at[1, i])
        arrived(above, 0)
        share(above, s_x.at[0, i])

    for n in range(3):
        arrived(4, n)
        push(4, n, 4 + y - y_up, s_y.at[0, n], to_y_up)
        push(4, n, 4 + y - y_down, s_y.at[1, n], to_y_down)
        if n < 2:
            z_sends(4, y, 0, n)

    @pl.when(c == 1)
    def _():
        give_core(4)

    shape = (RT * RT, SLOTS)
    places = lax.broadcasted_iota(jnp.int32, shape, 0)
    numbers = lax.broadcasted_iota(jnp.int32, shape, 1)
    lanes = lax.broadcasted_iota(jnp.int32, (RT * RT, TILE), 1)
    found = jnp.full((RT * RT, TILE), STEPS * SLOTS, jnp.int32)
    for step in range(STEPS):
        names = tile_rows[step : step + 1, :] * RT + tile_cols[step : step + 1, :]
        hit = jnp.logical_and(names == places, numbers < counts[0, step])
        best = jnp.min(jnp.where(hit, numbers + step * SLOTS, STEPS * SLOTS), axis=1, keepdims=True)
        found = jnp.where(lanes == step, best, found)
    table[...] = found
    table_copy = pltpu.make_async_copy(table, slots, table_sem)
    table_copy.start()

    from_up = 4 + y_up - y
    from_down = 4 + y_down - y
    for n in range(3):
        if n == 0:
            arrived(8, 0)
            push(8, 0, 12, s_rd, to_z_down)
        if n == 1:
            arrived(0, 1)
            push(0, 1, 12, s_ru, device(k, at(z + 5, y), c))
        arrived(from_down, n)
        if n != 1:
            push(from_down, n, 4 + y_down - y_up, s_yr.at[n], to_y_up)
        if n == 0:
            z_sends(from_down, y_down, 3, n)
        arrived(from_up, n)
        if n == 1:
            push(from_up, n, 4 + y_up - y_down, s_yr.at[n], to_y_down)
        if n == 0:
            z_sends(from_up, y_up, 1, n)
        if n == 0:
            share(8, s_x.at[0, 0])
            arrived(0, 0)
            share(0, s_x.at[1, 0])

    @pl.when(c == 1)
    def _():
        give_core(from_up)
        give_core(from_down)

    opposite = (y + 2) % 4
    from_opposite = 4 + opposite - y
    arrived(from_opposite, 0)
    z_sends(from_opposite, opposite, 2, 0)
    z_sends(from_down, y_down, 3, 1)
    z_sends(from_up, y_up, 1, 1)
    arrived(from_opposite, 1)
    z_sends(from_opposite, opposite, 2, 1)
    arrived(from_opposite, 2)

    @pl.when(c == 1)
    def _():
        give_core(from_opposite)

    far_up = 12 + y_up - y
    far_down = 12 + y_down - y
    far_opposite = 12 + opposite - y

    def far_spread(n):
        arrived(12, n)
        push(12, n, 12 + y - y_up, s_fy.at[0, n], to_y_up)
        push(12, n, 12 + y - y_down, s_fy.at[1, n], to_y_down)

    far_spread(0)
    share(12, s_x2.at[0])
    turn_corner(y_up - y, 1, 0)
    turn_corner(y_down - y, 3, 0)
    share_edge(y_up - y, 1)
    share_edge(y_down - y, 3)

    acc[...] = jnp.zeros_like(acc)
    table_copy.wait()
    for step in range(STEPS):
        pltpu.make_async_copy(
            weights.at[pl.ds(step * SLOTS, SLOTS)], wbuf.at[pl.ds(step * SLOTS, SLOTS)], w_sem.at[step]
        ).wait()

    group = 6

    def multiply(slot):
        step = slot % STEPS
        pltpu.make_async_copy(obuf.at[step], obuf.at[step], o_sem.at[step]).wait()
        half_cols = RT // 2

        def rows_of(r, carry):
            base = r * (group * RT)
            total = None
            for ref, at_slot, side in ((fbuf, slot, c), (obuf, step, 1 - c)):
                stacked = []
                for n in range(group):
                    tiles = [
                        wbuf[slots[base + n * RT + half_cols * side + i, step]] for i in range(half_cols)
                    ]
                    stacked.append(jnp.concatenate(tiles, axis=1))
                lhs = jnp.concatenate(stacked, axis=0)
                term = jnp.dot(lhs, ref[at_slot], preferred_element_type=jnp.float32)
                total = term if total is None else total + term
            window = pl.ds(pl.multiple_of(r * (group * TILE), group * TILE), group * TILE)
            acc[window, :] += total
            return carry

        lax.fori_loop(0, RT // group, rows_of, 0)

    def order(i):
        return i + i // 2 - 2 * (i // 3)

    def delta_of(i):
        return (y + order(i)) % 4 - y

    def early_pass(i, carry):
        multiply(4 + delta_of(i))
        return carry

    def far_pass(i, carry):
        far = 12 + delta_of(i)
        arrived(far, 2)

        @pl.when(c == 0)
        def _():
            give_core(far)

        @pl.when(c == 1)
        def _():
            multiply(far)

        return carry

    def late_pass(i, carry):
        delta = delta_of(i)
        above = 8 + delta
        below = (delta + 16) % 16

        @pl.when(i > 0)
        def _():
            arrived(below, 1)

        arrived(above, 1)
        arrived(above, 2)
        arrived(below, 2)
        mine = jnp.where(above // STEPS == c, above, below)
        theirs = above + below - mine
        give_core(theirs)
        multiply(mine)
        return carry

    far_spread(1)
    arrived(far_down, 0)
    push(far_down, 0, 12 + y_down - y_up, s_fyr.at[0], to_y_up)
    share(far_down, s_x2.at[3])
    arrived(far_up, 0)
    share(far_up, s_x2.at[1])
    turn_corner(opposite - y, 2, 0)
    share_edge(opposite - y, 2)

    @pl.when(c == 0)
    def _():
        lax.fori_loop(0, 2, early_pass, 0)

    turn_corner(y_up - y, 1, 1)
    turn_corner(y_down - y, 3, 1)
    arrived(far_up, 1)
    push(far_up, 1, 12 + y_up - y_down, s_fyr.at[1], to_y_down)
    arrived(far_opposite, 0)
    share(far_opposite, s_x2.at[2])

    @pl.when(c == 0)
    def _():
        lax.fori_loop(2, 4, early_pass, 0)

    lax.fori_loop(0, 1, late_pass, 0)
    turn_corner(opposite - y, 2, 1)
    lax.fori_loop(0, 1, far_pass, 0)
    arrived(far_down, 1)
    lax.fori_loop(1, 2, late_pass, 0)
    arrived(far_opposite, 1)
    lax.fori_loop(1, 4, far_pass, 0)
    lax.fori_loop(2, 4, late_pass, 0)

    for part in (1 - k, k):
        start = pl.multiple_of((2 * part + 1 - c) * QUARTER, QUARTER)
        pltpu.make_async_remote_copy(
            src_ref=acc.at[pl.ds(start, QUARTER)],
            dst_ref=r1buf.at[part],
            send_sem=s_r1.at[part],
            recv_sem=r1_sem.at[part],
            device_id=other_core,
            device_id_type=MESH,
        ).start()

    def r1_arrived(part):
        pltpu.make_async_copy(r1buf.at[part], r1buf.at[part], r1_sem.at[part]).wait()

    away = pl.multiple_of((2 * (1 - k) + c) * QUARTER, QUARTER)
    r1_arrived(1 - k)
    r2src[...] = (acc[pl.ds(away, QUARTER), :] + r1buf[1 - k]).astype(r2src.dtype)
    cross = pltpu.make_async_remote_copy(
        src_ref=r2src,
        dst_ref=r2buf,
        send_sem=s_r2,
        recv_sem=r2_sem,
        device_id=to_rep,
        device_id_type=MESH,
    )
    cross.start()
    r1_arrived(k)
    home = pl.multiple_of((2 * k + c) * QUARTER, QUARTER)
    kept = acc[pl.ds(home, QUARTER), :] + r1buf[k]
    own = features.reshape(ROWS, WIDTH)[pl.ds(home, QUARTER), :]
    pre = jnp.dot(own, weight_self[...], preferred_element_type=jnp.float32)
    cross.wait()
    aggregate = (kept + r2buf[...].astype(jnp.float32)).astype(jnp.bfloat16)
    pre = pre + jnp.dot(aggregate, weight_neigh[...], preferred_element_type=jnp.float32)
    sigmoid = jax.nn.sigmoid(pre)
    out_ref[...] = (pre * sigmoid).astype(out_ref.dtype)
    slope = (cotangent[...].astype(jnp.float32) * sigmoid * (1.0 + pre * (1.0 - sigmoid))).astype(
        jnp.bfloat16
    )
    contract = (((0,), (0,)), ((), ()))
    self_term = lax.dot_general(own, slope, contract, preferred_element_type=jnp.float32)
    neigh_term = lax.dot_general(aggregate, slope, contract, preferred_element_type=jnp.float32)
    gsrc[...] = jnp.where(c == 0, neigh_term, self_term)
    core_swap = pltpu.make_async_remote_copy(
        src_ref=gsrc,
        dst_ref=gin,
        send_sem=s_g0,
        recv_sem=g0_sem,
        device_id=other_core,
        device_id_type=MESH,
    )
    core_swap.start()
    for part in range(2):
        pltpu.make_async_copy(r1buf.at[part], r1buf.at[part], s_r1.at[part]).wait()
    core_swap.wait()
    chip_term = jnp.where(c == 0, self_term, neigh_term) + gin[...]
    for side in range(2):
        gsum[:, side] = chip_term[:, side * TILE : (side + 1) * TILE].reshape(CHIPS // 2, 8, TILE)
    me = 32 * k + g

    def scatter(t, carry):
        peer = (me + t) % CHIPS
        pltpu.make_async_remote_copy(
            src_ref=gsum.at[peer // 2, peer % 2],
            dst_ref=rsbuf.at[t - 1],
            send_sem=s_rs,
            recv_sem=rs_sem,
            device_id=device(peer // 32, peer % 32, c),
            device_id_type=MESH,
        ).start()
        return carry

    lax.fori_loop(1, CHIPS, scatter, 0)
    everything = pltpu.make_async_copy(rsbuf, rsbuf, rs_sem)
    everything.wait()
    piece = gsum[me // 2, me % 2] + jnp.sum(rsbuf[...], axis=0)
    agbuf[me // 2, me % 2] = piece.astype(agbuf.dtype)

    def gather(t, carry):
        peer = (me + t) % CHIPS
        pltpu.make_async_remote_copy(
            src_ref=agbuf.at[me // 2, me % 2],
            dst_ref=agbuf.at[me // 2, me % 2],
            send_sem=s_ag,
            recv_sem=ag_sem,
            device_id=device(peer // 32, peer % 32, c),
            device_id_type=MESH,
        ).start()
        return carry

    lax.fori_loop(1, CHIPS, gather, 0)

    for n in range(3):
        sent(s_y.at[0, n], n)
        sent(s_y.at[1, n], n)
        sent(s_yr.at[n], n)
    for j in range(4):
        for n in range(2):
            sent(s_zd.at[j, n], n)
            sent(s_zu.at[j, n], n)

            @pl.when(turns(edge_high, (y + j) % 4 - y, j, n))
            def _():
                sent(s_t.at[j, n], n)

            sent(s_x.at[n, j], 0)
        sent(s_x2.at[j], 0)
    sent(s_rd, 0)
    sent(s_ru, 1)
    for n in range(2):
        sent(s_fy.at[0, n], n)
        sent(s_fy.at[1, n], n)
        sent(s_fyr.at[n], n)
    for step in range(STEPS):
        pltpu.make_async_copy(obuf.at[step], obuf.at[step], s_o.at[step]).wait()

    @pl.when(sender)
    def _():
        for number, start, size in cuts:
            here = fbuf.at[4, pl.ds(start, size)]
            pltpu.make_async_copy(here, here, s_swap.at[number]).wait()

    pltpu.make_async_copy(rsbuf, rsbuf, s_rs).wait()
    came_in = agbuf.reshape(CHIPS, 8, TILE).at[pl.ds(0, CHIPS - 1)]
    pltpu.make_async_copy(came_in, came_in, ag_sem).wait()
    last = pltpu.make_async_remote_copy(
        src_ref=agbuf,
        dst_ref=agother,
        send_sem=s_g1,
        recv_sem=g1_sem,
        device_id=other_core,
        device_id_type=MESH,
    )
    last.start()
    pltpu.make_async_copy(came_in, came_in, s_ag).wait()
    last.wait()
    held = agbuf[...].astype(jnp.float32)
    came = agother[...].astype(jnp.float32)
    self_ref[...] = jnp.where(c == 0, held, came)
    neigh_ref[...] = jnp.where(c == 0, came, held)


def finish_kernel(out_in, self_in, neigh_in, out_ref, self_ref, neigh_ref):
    out_ref[...] = out_in[...]
    for side in range(2):
        lanes = slice(side * TILE, (side + 1) * TILE)
        self_ref[:, lanes] = self_in[:, side].reshape(WIDTH, TILE)
        neigh_ref[:, lanes] = neigh_in[:, side].reshape(WIDTH, TILE)


def on_device(
    features, tile_weights, tile_rows, tile_cols, tile_counts, weight_self, weight_neigh, cotangent
):
    weights = tile_weights.reshape(STEPS * SLOTS, TILE, TILE)
    vmem = pl.BlockSpec(memory_space=pltpu.VMEM)
    dma = pltpu.SemaphoreType.DMA
    raw = pl.pallas_call(
        aggregate_kernel,
        out_shape=(
            jax.ShapeDtypeStruct((QUARTER, WIDTH), jnp.bfloat16),
            jax.ShapeDtypeStruct((CHIPS // 2, 2, 8, TILE), jnp.float32),
            jax.ShapeDtypeStruct((CHIPS // 2, 2, 8, TILE), jnp.float32),
        ),
        in_specs=[
            pl.BlockSpec(memory_space=pltpu.SMEM),
            vmem,
            vmem,
            vmem,
            pl.BlockSpec(memory_space=pl.ANY),
            vmem,
            vmem,
            vmem,
        ],
        out_specs=(vmem, vmem, vmem),
        scratch_shapes=[
            pltpu.VMEM((STEPS * SLOTS + 1, TILE, TILE), jnp.bfloat16),
            pltpu.VMEM((2 * STEPS, HALF, WIDTH), jnp.bfloat16),
            pltpu.VMEM((STEPS, HALF, WIDTH), jnp.bfloat16),
            pltpu.VMEM((ROWS, WIDTH), jnp.float32),
            pltpu.VMEM((2, QUARTER, WIDTH), jnp.float32),
            pltpu.VMEM((QUARTER, WIDTH), jnp.bfloat16),
            pltpu.VMEM((QUARTER, WIDTH), jnp.bfloat16),
            dma((STEPS,)),
            dma((1,)),
            dma((2 * STEPS, 3)),
            dma((STEPS,)),
            dma((2,)),
            dma,
            dma((3,)),
            dma((2, 3)),
            dma((3,)),
            dma((4, 2)),
            dma((4, 2)),
            dma,
            dma,
            dma((2, 4)),
            dma((4,)),
            dma((STEPS,)),
            dma((2,)),
            dma,
            pltpu.VMEM((WIDTH, WIDTH), jnp.float32),
            pltpu.VMEM((WIDTH, WIDTH), jnp.float32),
            pltpu.VMEM((CHIPS // 2, 2, 8, TILE), jnp.float32),
            pltpu.VMEM((CHIPS - 1, 8, TILE), jnp.float32),
            pltpu.VMEM((CHIPS // 2, 2, 8, TILE), jnp.bfloat16),
            pltpu.VMEM((CHIPS // 2, 2, 8, TILE), jnp.bfloat16),
            dma,
            dma,
            dma,
            dma,
            dma,
            dma,
            dma,
            dma,
            pltpu.VMEM((4, HALF, WIDTH), jnp.bfloat16),
            dma((4, 2)),
            dma((4, 2)),
            dma((2, 2)),
            dma((2,)),
            pltpu.VMEM((RT * RT, TILE), jnp.int32),
            pltpu.SMEM((RT * RT, TILE), jnp.int32),
            dma,
        ],
        compiler_params=pltpu.CompilerParams(
            collective_id=0, has_side_effects=True, vmem_limit_bytes=60 * 1024 * 1024
        ),
    )(
        tile_counts.reshape(1, STEPS),
        tile_rows.reshape(STEPS, SLOTS),
        tile_cols.reshape(STEPS, SLOTS),
        features.reshape(2, HALF, WIDTH),
        weights,
        weight_self,
        weight_neigh,
        cotangent,
    )
    return pl.pallas_call(
        finish_kernel,
        out_shape=(
            jax.ShapeDtypeStruct((QUARTER, WIDTH), jnp.bfloat16),
            jax.ShapeDtypeStruct((WIDTH, WIDTH), jnp.float32),
            jax.ShapeDtypeStruct((WIDTH, WIDTH), jnp.float32),
        ),
        in_specs=[vmem, vmem, vmem],
        out_specs=(vmem, vmem, vmem),
    )(*raw)


def solution(mesh):
    return jax.shard_map(
        on_device,
        mesh=mesh,
        in_specs=(
            P("dom", None),
            P("dom", "rep", None, None, None, None),
            P("dom", "rep", None, None),
            P("dom", "rep", None, None),
            P("dom", "rep", None),
            P(),
            P(),
            P(("dom", "rep"), None),
        ),
        out_specs=(P(("dom", "rep"), None), P(), P()),
        check_vma=False,
    )
```
